256 devices in a mesh: tm: 16 (over x, y), space: 16 (over z, core).
Axes of the slice: x: 4, y: 4, z: 8, core: 2. Of those that a mesh axis runs over, the one named last changes fastest.
Arguments:
- clip: bfloat16 [256, 512, 768], P('tm', 'space'), may hold values from -160 to 160
- w_spatial: bfloat16 [4, 768, 768], replicated, may hold values from -4 to 4
- w_temporal: bfloat16 [4, 768, 768], replicated, may hold values from -4 to 4
Outputs:
- result: bfloat16 [256, 512, 768], P('tm', 'space')
The draws below stay inside these ranges and needn't reach their ends.
All inputs are finite; a program needn't handle non-finite values.
Results may differ from the reference program's by a relative error of at most 0.011.
Values may be sent and summed in bfloat16 or wider, within the bound.
A program may use at most 128 MiB of HBM per device.

```python
import math
import jax
import jax.numpy as jnp
from jax import lax

D = 768
HEAD = 64
HEADS = 12
FRAMES = 256
TOKS = 512


def scaled_normal(key, shape, limit):
    return jnp.clip(jax.random.normal(key, shape, jnp.float32), -limit, limit)


def draw_clip(key, part):
    keys = jax.random.split(jax.random.fold_in(key, 11), 3)
    column = jnp.exp(jax.random.uniform(keys[0], (D,), jnp.float32, 0.0, math.log(10.0)))
    column = column / jnp.sqrt(jnp.mean(column * column))
    row_scale = jnp.exp(jax.random.uniform(keys[1], (FRAMES, TOKS, 1), jnp.float32, math.log(0.3), math.log(3.0)))
    values = scaled_normal(keys[2], (FRAMES, TOKS, D), 5.0)
    return (values * column[None, None, :] * row_scale).astype(jnp.bfloat16)


def attention_weights(key, salt):
    keys = jax.random.split(jax.random.fold_in(key, salt), 1)
    drawn = scaled_normal(keys[0], (4, D, D), 4.0) / math.sqrt(D)
    return drawn.astype(jnp.bfloat16)


def draw_w_spatial(key, part):
    return attention_weights(key, 23)


def draw_w_temporal(key, part):
    return attention_weights(key, 37)


def setup_inputs(seed: int = 0) -> dict:
    streams_of = jax.random.split(jax.random.key(seed), 4)
    clip = draw_clip(jax.random.fold_in(streams_of[3], 71), 0)
    w_spatial = draw_w_spatial(jax.random.fold_in(streams_of[3], 71), 0)
    w_temporal = draw_w_temporal(jax.random.fold_in(streams_of[3], 71), 0)
    return dict(clip=clip, w_spatial=w_spatial, w_temporal=w_temporal)


def rms_norm(values):
    wide = values.astype(jnp.float32)
    return (wide * lax.rsqrt(lax.optimization_barrier(jnp.mean(wide * wide, axis=-1, keepdims=True)) + 1e-06)).astype(jnp.bfloat16)

def project_three(normed, weights):
    flat = normed.reshape(-1, D)
    outs = []
    for index in range(3):
        outs.append(jnp.dot(flat, weights[index], preferred_element_type=jnp.float32).astype(jnp.bfloat16).reshape(normed.shape))
    return outs

def frame_attend(parts):
    query, key, value = parts
    qh = query.astype(jnp.float32).reshape(TOKS, HEADS, HEAD)
    kh = key.astype(jnp.float32).reshape(TOKS, HEADS, HEAD)
    vh = value.astype(jnp.float32).reshape(TOKS, HEADS, HEAD)
    scores = jnp.einsum('qhd,khd->hqk', qh, kh) / jnp.sqrt(jnp.float32(HEAD))
    weights = jax.nn.softmax(scores, axis=-1).astype(jnp.bfloat16)
    mixed = jnp.einsum('hqk,khd->qhd', weights.astype(jnp.float32), vh)
    return mixed.astype(jnp.bfloat16).reshape(TOKS, D)

def series_attend(parts):
    query, key, value = parts
    qh = query.astype(jnp.float32).reshape(FRAMES, HEADS, HEAD)
    kh = key.astype(jnp.float32).reshape(FRAMES, HEADS, HEAD)
    vh = value.astype(jnp.float32).reshape(FRAMES, HEADS, HEAD)
    scores = jnp.einsum('fhd,ghd->hfg', qh, kh) / jnp.sqrt(jnp.float32(HEAD))
    order = jnp.arange(FRAMES, dtype=jnp.int32)
    allowed = order[None, :] <= order[:, None]
    scores = jnp.where(allowed[None], scores, -jnp.inf)
    weights = jax.nn.softmax(scores, axis=-1)
    mixed = jnp.einsum('hfg,ghd->fhd', weights, vh)
    return mixed.astype(jnp.bfloat16).reshape(FRAMES, D)

def out_project(mixed, weight):
    return jnp.dot(mixed.reshape(-1, D), weight, preferred_element_type=jnp.float32).reshape(mixed.shape)

def reference(clip, w_spatial, w_temporal):
    normed = rms_norm(clip)
    sq, sk, sv = project_three(normed, w_spatial)
    smix = lax.map(frame_attend, (sq, sk, sv))
    after_space = (clip.astype(jnp.float32) + out_project(smix, w_spatial[3])).astype(jnp.bfloat16)
    tnormed = rms_norm(after_space)
    tq, tk, tv = project_three(tnormed, w_temporal)
    tmix = lax.map(series_attend, (jnp.swapaxes(tq, 0, 1), jnp.swapaxes(tk, 0, 1), jnp.swapaxes(tv, 0, 1)))
    tmix = jnp.swapaxes(tmix, 0, 1)
    return (after_space.astype(jnp.float32) + out_project(tmix, w_temporal[3])).astype(jnp.bfloat16)
```

```python
import functools
import math

import jax
import jax.numpy as jnp
from jax import lax
from jax.experimental import pallas as pl
from jax.experimental.pallas import tpu as pltpu
from jax.sharding import PartitionSpec as P

MESH = pl.DeviceIdType.MESH
HEAD = 64
LANES = 128
WIDTH = 768
PAIRS = WIDTH // LANES
SCALE = math.log2(math.e) / math.sqrt(HEAD)
BF16 = jnp.bfloat16
F32 = jnp.float32

Z_OFFS = [(0, 0), (0, 1)]
for _far in (1, -1, 2, -2, 3, -3, 4):
    Z_OFFS += [(_far, 0), (_far, 1)]
Z_INV = [Z_OFFS.index((dz if dz == 4 else -dz, dc)) for dz, dc in Z_OFFS]
T_OFFS = [(dx, dy) for dx in (0, 1, 3, 2) for dy in (0, 1, 3, 2)]
T_INV = [T_OFFS.index(((-dx) % 4, (-dy) % 4)) for dx, dy in T_OFFS]

Z_GROUPS = ((0, 2), (2, 6), (6, 10), (10, 14), (14, 16))
A_SENDS = list(range(15, 0, -1))


def z_peer(me, slot):
    dz, dc = Z_OFFS[slot]
    return lax.rem(me // 2 + (dz + 8), 8) * 2 + lax.rem(lax.rem(me, 2) + dc, 2)


def t_peer(me, slot):
    dx, dy = T_OFFS[slot]
    return lax.rem(me // 4 + dx, 4) * 4 + lax.rem(lax.rem(me, 4) + dy, 4)


def normed_rows(rows):
    wide = rows.astype(F32)
    return (wide * lax.rsqrt(jnp.mean(wide * wide, axis=-1, keepdims=True) + 1e-06)).astype(BF16)


def dot(a, b):
    return jnp.dot(a, b, preferred_element_type=F32)


def attend(q, k, vx, mask):
    n = q.shape[0] // 2
    scores = lax.dot_general(q, k, (((1,), (1,)), ((), ())), preferred_element_type=F32)
    if mask is not None:
        scores = jnp.where(mask, scores, -1e30)
    largest = jnp.max(scores, axis=-1, keepdims=True)
    expo = jnp.exp2(scores - largest).astype(BF16)
    both = dot(expo, vx)
    both = both[:, :LANES] / both[:, LANES:]
    lane = lax.broadcasted_iota(jnp.int32, (n, LANES), 1)
    return jnp.where(lane < HEAD, both[:n], both[n:]).astype(BF16)


def kernel(
    clip, w_space, w_time, out,
    ws, wt, x, q2, k, vx, mix, after, home, perm, grouped, series,
    tq2, tk, tvx, tmix, answer, back, final,
    w_sem, a_send, a_recv, b_send, b_recv, c_send, c_recv, d_send, d_recv, own_sem, out_sem,
):
    t_me = lax.axis_index("tm")
    s_me = lax.axis_index("space")

    loads = [pltpu.make_async_copy(w_space, ws, w_sem.at[0]), pltpu.make_async_copy(w_time, wt, w_sem.at[1])]
    own_a = pltpu.make_async_copy(clip.at[s_me], x.at[0], own_sem.at[0])
    own_a.start()
    for load in loads:
        load.start()

    barrier = pltpu.get_barrier_semaphore()
    for slot in range(1, 16):
        pl.semaphore_signal(barrier, inc=1, device_id={"space": z_peer(s_me, slot)}, device_id_type=MESH)
        pl.semaphore_signal(barrier, inc=1, device_id={"tm": t_peer(t_me, slot)}, device_id_type=MESH)
    pl.semaphore_wait(barrier, 30)

    def a_copy(slot):
        peer = z_peer(s_me, slot)
        return pltpu.make_async_remote_copy(
            src_ref=clip.at[peer], dst_ref=x.at[Z_INV[slot]],
            send_sem=a_send.at[slot], recv_sem=a_recv.at[Z_INV[slot]],
            device_id={"space": peer}, device_id_type=MESH,
        )

    for slot in A_SENDS:
        a_copy(slot).start()

    ones = jnp.ones((512, LANES), BF16)
    for pair in range(PAIRS):
        vx[pair, :, LANES:] = ones
        tvx[pair, :, LANES:] = ones[:256]
    row = lax.broadcasted_iota(jnp.int32, (256, 256), 0)
    col = lax.broadcasted_iota(jnp.int32, (256, 256), 1)
    swap = (row // 16 == col % 16) & (row % 16 == col // 16)
    perm[...] = jnp.where(swap, 1.0, 0.0).astype(BF16)
    lane = lax.broadcasted_iota(jnp.int32, (1, WIDTH), 1)
    first = jnp.where(lane % LANES < HEAD, SCALE, 0.0).astype(F32)
    second = jnp.where(lane % LANES < HEAD, 0.0, SCALE).astype(F32)

    loads[0].wait()
    own_a.wait()
    for lo, hi in Z_GROUPS:
        for slot in range(max(lo, 1), hi):
            pltpu.make_async_remote_copy(
                src_ref=clip.at[0], dst_ref=x.at[slot], send_sem=a_send.at[slot], recv_sem=a_recv.at[slot],
                device_id={"space": z_peer(s_me, slot)}, device_id_type=MESH,
            ).wait_recv()
        count = hi - lo
        normed = normed_rows(x[lo:hi].reshape(count * 32, WIDTH))
        for index in range(3):
            made = dot(normed, ws[index])
            if index == 0:
                kinds = [((made * first).astype(BF16), q2, 0), ((made * second).astype(BF16), q2, 1)]
            else:
                kinds = [(made.astype(BF16), (k, vx)[index - 1], None)]
            for value, ref, head in kinds:
                value = value.reshape(count, 2, 16, WIDTH)
                for th in range(2):
                    part = value[:, th].reshape(count * 16, WIDTH)
                    at = pl.ds(th * 256 + lo * 16, count * 16)
                    for pair in range(PAIRS):
                        piece = part[:, pair * LANES:(pair + 1) * LANES]
                        if head is None:
                            ref[pair, at, :LANES] = piece
                        else:
                            ref[pair, head, at, :] = piece

    def b_copy(th, slot):
        peer = z_peer(s_me, slot)
        return pltpu.make_async_remote_copy(
            src_ref=after.at[th, slot], dst_ref=home.at[th, s_me],
            send_sem=b_send.at[th, slot], recv_sem=b_recv.at[th, Z_INV[slot]],
            device_id={"space": peer}, device_id_type=MESH,
        )

    def c_copy(th, slot):
        peer = t_peer(t_me, slot)
        return pltpu.make_async_remote_copy(
            src_ref=grouped.at[th, peer], dst_ref=series.at[th, t_me],
            send_sem=c_send.at[th, slot], recv_sem=c_recv.at[th, T_INV[slot]],
            device_id={"tm": peer}, device_id_type=MESH,
        )

    def d_copy(th, slot):
        peer = t_peer(t_me, slot)
        return pltpu.make_async_remote_copy(
            src_ref=answer.at[th, peer], dst_ref=back.at[th, t_me],
            send_sem=d_send.at[th, slot], recv_sem=d_recv.at[th, T_INV[slot]],
            device_id={"tm": peer}, device_id_type=MESH,
        )

    own_b = [pltpu.make_async_copy(after.at[th, 0], home.at[th, s_me], own_sem.at[1 + th]) for th in range(2)]
    own_c = [pltpu.make_async_copy(grouped.at[th, t_me], series.at[th, t_me], own_sem.at[3 + th]) for th in range(2)]
    own_d = [pltpu.make_async_copy(answer.at[th, t_me], back.at[th, t_me], own_sem.at[5 + th]) for th in range(2)]

    def space_block(th, half):
        base = th * 256 + half * 128

        def one(pair, carry):
            q = q2[pair, :, base:base + 128, :].reshape(256, LANES)
            mixed = attend(q, k[pair], vx[pair], None)
            mix[:, pl.ds(pl.multiple_of(pair * LANES, LANES), LANES)] = mixed
            return carry

        lax.fori_loop(0, PAIRS, one, 0)
        held = x[half * 8:half * 8 + 8, th * 16:th * 16 + 16, :].reshape(128, WIDTH).astype(F32)
        done = (held + dot(mix[...], ws[3])).astype(BF16)
        after[th, half * 8:half * 8 + 8] = done.reshape(8, 16, WIDTH)
        for slot in range(half * 8 + 7, half * 8 - 1, -1):
            if slot == 0:
                own_b[th].start()
            else:
                b_copy(th, slot).start()

    def regroup(th):
        own_b[th].wait()
        for slot in range(1, 16):
            pltpu.make_async_remote_copy(
                src_ref=after.at[th, slot], dst_ref=home.at[th, z_peer(s_me, slot)],
                send_sem=b_send.at[th, slot], recv_sem=b_recv.at[th, slot],
                device_id={"space": z_peer(s_me, slot)}, device_id_type=MESH,
            ).wait_recv()
        moved = dot(perm[...], home[th].reshape(256, WIDTH)).astype(BF16)
        grouped[th] = moved.reshape(16, 16, WIDTH)
        own_c[th].start()
        for slot in range(1, 16):
            c_copy(th, slot).start()

    def time_project(th):
        own_c[th].wait()
        for slot in range(1, 16):
            pltpu.make_async_remote_copy(
                src_ref=grouped.at[th, 0], dst_ref=series.at[th, t_peer(t_me, slot)],
                send_sem=c_send.at[th, slot], recv_sem=c_recv.at[th, slot],
                device_id={"tm": t_peer(t_me, slot)}, device_id_type=MESH,
            ).wait_recv()
        normed = normed_rows(series[th].reshape(256, WIDTH))
        for index in range(3):
            made = dot(normed, wt[index])
            for pair in range(PAIRS):
                cols = slice(pair * LANES, (pair + 1) * LANES)
                if index == 0:
                    tq2[pair, 0] = (made[:, cols] * first[:, cols]).astype(BF16)
                    tq2[pair, 1] = (made[:, cols] * second[:, cols]).astype(BF16)
                elif index == 1:
                    tk[pair] = made[:, cols].astype(BF16)
                else:
                    tvx[pair, :, :LANES] = made[:, cols].astype(BF16)

    def time_block(th, half):
        keys = 128 * (half + 1)
        query = lax.broadcasted_iota(jnp.int32, (256, keys), 0) % 128 + 128 * half
        mask = lax.broadcasted_iota(jnp.int32, (256, keys), 1) <= query

        def one(pair, carry):
            q = tq2[pair, :, half * 128:half * 128 + 128, :].reshape(256, LANES)
            mixed = attend(q, tk[pair, :keys, :], tvx[pair, :keys, :], mask)
            tmix[:, pl.ds(pl.multiple_of(pair * LANES, LANES), LANES)] = mixed
            return carry

        lax.fori_loop(0, PAIRS, one, 0)
        held = series[th, half * 8:half * 8 + 8].reshape(128, WIDTH).astype(F32)
        done = (held + dot(tmix[...], wt[3])).astype(BF16)
        answer[th, half * 8:half * 8 + 8] = done.reshape(8, 16, WIDTH)

    def send_answer(th):
        own_d[th].start()
        for slot in range(1, 16):
            d_copy(th, slot).start()

    outs = [
        pltpu.make_async_copy(final.at[th], out.at[:, pl.ds(th * 16, 16), :], out_sem.at[th]) for th in range(2)
    ]

    def finish(th):
        own_d[th].wait()
        for slot in range(1, 16):
            pltpu.make_async_remote_copy(
                src_ref=answer.at[th, 0], dst_ref=back.at[th, t_peer(t_me, slot)],
                send_sem=d_send.at[th, slot], recv_sem=d_recv.at[th, slot],
                device_id={"tm": t_peer(t_me, slot)}, device_id_type=MESH,
            ).wait_recv()
        moved = dot(perm[...], back[th].reshape(256, WIDTH)).astype(BF16)
        final[th] = moved.reshape(16, 16, WIDTH)
        outs[th].start()

    for th in range(2):
        space_block(th, 1)
        space_block(th, 0)
    regroup(0)
    loads[1].wait()
    time_project(0)
    time_block(0, 0)
    time_block(0, 1)
    regroup(1)
    send_answer(0)
    time_project(1)
    time_block(1, 0)
    time_block(1, 1)
    send_answer(1)
    finish(0)
    finish(1)

    for slot in range(1, 16):
        a_copy(slot).wait_send()
        for th in range(2):
            b_copy(th, slot).wait_send()
            c_copy(th, slot).wait_send()
            d_copy(th, slot).wait_send()
    for copy in outs:
        copy.wait()


def on_device(clip, w_spatial, w_temporal):
    dma = pltpu.SemaphoreType.DMA
    vmem = pltpu.VMEM
    return pl.pallas_call(
        kernel,
        out_shape=jax.ShapeDtypeStruct(clip.shape, BF16),
        in_specs=[pl.BlockSpec(memory_space=pl.ANY)] * 3,
        out_specs=pl.BlockSpec(memory_space=pl.ANY),
        scratch_shapes=[
            vmem((4, WIDTH, WIDTH), BF16),
            vmem((4, WIDTH, WIDTH), BF16),
            vmem((16, 32, WIDTH), BF16),
            vmem((PAIRS, 2, 512, LANES), BF16),
            vmem((PAIRS, 512, LANES), BF16),
            vmem((PAIRS, 512, 2 * LANES), BF16),
            vmem((128, WIDTH), BF16),
            vmem((2, 16, 16, WIDTH), BF16),
            vmem((2, 16, 16, WIDTH), BF16),
            vmem((256, 256), BF16),
            vmem((2, 16, 16, WIDTH), BF16),
            vmem((2, 16, 16, WIDTH), BF16),
            vmem((PAIRS, 2, 256, LANES), BF16),
            vmem((PAIRS, 256, LANES), BF16),
            vmem((PAIRS, 256, 2 * LANES), BF16),
            vmem((128, WIDTH), BF16),
            vmem((2, 16, 16, WIDTH), BF16),
            vmem((2, 16, 16, WIDTH), BF16),
            vmem((2, 16, 16, WIDTH), BF16),
            dma((2,)),
            dma((16,)), dma((16,)),
            dma((2, 16)), dma((2, 16)),
            dma((2, 16)), dma((2, 16)),
            dma((2, 16)), dma((2, 16)),
            dma((7,)),
            dma((2,)),
        ],
        compiler_params=pltpu.CompilerParams(
            collective_id=0, has_side_effects=True, vmem_limit_bytes=60 * 1024 * 1024
        ),
    )(clip, w_spatial, w_temporal)


def solution(mesh):
    placed = (P("tm", "space", None), P(), P())
    return jax.shard_map(
        on_device, mesh=mesh, in_specs=placed, out_specs=P("tm", "space", None), check_vma=False
    )
```

```python
import functools
import math

import jax
import jax.numpy as jnp
from jax import lax
from jax.experimental import pallas as pl
from jax.experimental.pallas import tpu as pltpu
from jax.sharding import PartitionSpec as P

MESH = pl.DeviceIdType.MESH
HEAD = 64
LANES = 128
WIDTH = 768
PAIRS = WIDTH // LANES
SCALE = math.log2(math.e) / math.sqrt(HEAD)
BF16 = jnp.bfloat16
F32 = jnp.float32

Z_OFFS = [(dz, dc) for dz in (3, -3, 1, -1, 0, 2, -2, 4) for dc in (0, 1)]
OWN = 8
OTHERS = [slot for slot in range(16) if slot != OWN]
Z_INV = [Z_OFFS.index((dz if dz == 4 else -dz, dc)) for dz, dc in Z_OFFS]
T_OFFS = [(dx, dy) for dx in (0, 1, 3, 2) for dy in (0, 1, 3, 2)]
T_INV = [T_OFFS.index(((-dx) % 4, (-dy) % 4)) for dx, dy in T_OFFS]

A_SENDS = (9, 14, 15, 0, 2, 1, 3, 10, 12, 11, 13, 4, 6, 5, 7)
B_SENDS = ((0, 2, 1, 3, 4, 6, 5, 7), (14, 15, 10, 12, 11, 13, 9, 8))
Z_GROUPS = ((8, 10), (14, 16), (0, 4), (10, 14), (4, 8))


def z_peer(me, slot):
    dz, dc = Z_OFFS[slot]
    return lax.rem(me // 2 + (dz + 8), 8) * 2 + lax.rem(lax.rem(me, 2) + dc, 2)


def t_peer(me, slot):
    dx, dy = T_OFFS[slot]
    return lax.rem(me // 4 + dx, 4) * 4 + lax.rem(lax.rem(me, 4) + dy, 4)


def normed_rows(rows):
    wide = rows.astype(F32)
    return (wide * lax.rsqrt(jnp.mean(wide * wide, axis=-1, keepdims=True) + 1e-06)).astype(BF16)


def dot(a, b):
    return jnp.dot(a, b, preferred_element_type=F32)


def attend(q, k, vx, bias):
    n = q.shape[0] // 2
    scores = lax.dot_general(q, k, (((1,), (1,)), ((), ())), preferred_element_type=F32)
    if bias is not None:
        scores = scores + bias
    largest = jnp.max(scores, axis=-1, keepdims=True)
    expo = jnp.exp2(scores - largest).astype(BF16)
    both = dot(expo, vx)
    both = both[:, :LANES] / both[:, LANES:]
    lane = lax.broadcasted_iota(jnp.int32, (n, LANES), 1)
    return jnp.where(lane < HEAD, both[:n], both[n:]).astype(BF16)


def kernel(
    clip, w_space, w_time, out,
    ws, wt, x, q2, k, vx, mix, after, home, perm, unperm, bias0, bias1, grouped, series,
    tq2, tk, tvx, tmix, answer, back, final,
    w_sem, a_send, a_recv, b_send, b_recv, c_send, c_recv, d_send, d_recv, own_sem, out_sem,
):
    t_me = lax.axis_index("tm")
    s_me = lax.axis_index("space")

    loads = [pltpu.make_async_copy(w_space, ws, w_sem.at[0]), pltpu.make_async_copy(w_time, wt, w_sem.at[1])]
    own_a = pltpu.make_async_copy(clip.at[s_me], x.at[OWN], own_sem.at[0])
    own_a.start()
    for load in loads:
        load.start()

    barrier = pltpu.get_barrier_semaphore()
    for slot in reversed(A_SENDS):
        pl.semaphore_signal(barrier, inc=1, device_id={"space": z_peer(s_me, slot)}, device_id_type=MESH)
    for slot in range(15, 0, -1):
        pl.semaphore_signal(barrier, inc=1, device_id={"tm": t_peer(t_me, slot)}, device_id_type=MESH)
    pl.semaphore_wait(barrier, 30)

    def a_copy(slot):
        peer = z_peer(s_me, slot)
        return pltpu.make_async_remote_copy(
            src_ref=clip.at[peer], dst_ref=x.at[Z_INV[slot]],
            send_sem=a_send.at[slot], recv_sem=a_recv.at[Z_INV[slot]],
            device_id={"space": peer}, device_id_type=MESH,
        )

    for slot in A_SENDS:
        a_copy(slot).start()

    ones = jnp.ones((512, LANES), BF16)
    for pair in range(PAIRS):
        vx[pair, :, LANES:] = ones
        tvx[pair, :, :, LANES:] = ones[:256].reshape(2, 128, LANES)
    frames = [z_peer(s_me, slot) for slot in range(16)]

    def frame_of(slots):
        found = jnp.zeros_like(slots)
        for slot in range(16):
            found = jnp.where(slots == slot, frames[slot], found)
        return found

    row = lax.broadcasted_iota(jnp.int32, (128, 128), 0)
    col = lax.broadcasted_iota(jnp.int32, (128, 128), 1)
    perm[...] = jnp.where((row // 8 == col % 16) & (row % 8 == col // 16), 1.0, 0.0).astype(BF16)
    row = lax.broadcasted_iota(jnp.int32, (256, 256), 0)
    col = lax.broadcasted_iota(jnp.int32, (1, 256), 1)
    unperm[...] = jnp.where((row // 16 == frame_of(col % 16)) & (row % 16 == col // 16), 1.0, 0.0).astype(BF16)
    for half, bias in enumerate((bias0, bias1)):
        blocks = 8 * (half + 1)
        key = lax.broadcasted_iota(jnp.int32, (1, 16 * blocks), 1)
        key_at = key % (8 * blocks) // 8 * 16 + frame_of(key // (8 * blocks) * 8 + key % 8)
        query = lax.broadcasted_iota(jnp.int32, (256, 1), 0) % 128
        query_at = (query % 64 // 8 + 8 * half) * 16 + frame_of(query // 64 * 8 + query % 8)
        bias[...] = jnp.where(key_at <= query_at, 0.0, -1e30).astype(F32)
    lane = lax.broadcasted_iota(jnp.int32, (1, WIDTH), 1)
    first = jnp.where(lane % LANES < HEAD, SCALE, 0.0).astype(F32)
    second = jnp.where(lane % LANES < HEAD, 0.0, SCALE).astype(F32)

    loads[0].wait()
    own_a.wait()
    for lo, hi in Z_GROUPS:
        for slot in range(lo, hi):
            if slot == OWN:
                continue
            pltpu.make_async_remote_copy(
                src_ref=clip.at[0], dst_ref=x.at[slot], send_sem=a_send.at[slot], recv_sem=a_recv.at[slot],
                device_id={"space": z_peer(s_me, slot)}, device_id_type=MESH,
            ).wait_recv()
        count = hi - lo
        normed = normed_rows(x[lo:hi].reshape(count * 32, WIDTH))
        for index in range(3):
            made = dot(normed, ws[index])
            if index == 0:
                kinds = [((made * first).astype(BF16), q2, 0), ((made * second).astype(BF16), q2, 1)]
            else:
                kinds = [(made.astype(BF16), (k, vx)[index - 1], None)]
            for value, ref, head in kinds:
                value = value.reshape(count, 2, 16, WIDTH)
                for th in range(2):
                    part = value[:, th].reshape(count * 16, WIDTH)
                    at = pl.ds(th * 256 + lo * 16, count * 16)
                    for pair in range(PAIRS):
                        piece = part[:, pair * LANES:(pair + 1) * LANES]
                        if head is None:
                            ref[pair, at, :LANES] = piece
                        else:
                            ref[pair, head, at, :] = piece

    def b_copy(th, slot):
        peer = z_peer(s_me, slot)
        return pltpu.make_async_remote_copy(
            src_ref=after.at[th, slot], dst_ref=home.at[th, Z_INV[slot]],
            send_sem=b_send.at[th, slot], recv_sem=b_recv.at[th, Z_INV[slot]],
            device_id={"space": peer}, device_id_type=MESH,
        )

    def c_copy(th, part, slot):
        peer = t_peer(t_me, slot)
        return pltpu.make_async_remote_copy(
            src_ref=grouped.at[th, part, peer], dst_ref=series.at[th, part, t_me],
            send_sem=c_send.at[th, part, slot], recv_sem=c_recv.at[th, part, T_INV[slot]],
            device_id={"tm": peer}, device_id_type=MESH,
        )

    def d_copy(th, slot):
        peer = t_peer(t_me, slot)
        return pltpu.make_async_remote_copy(
            src_ref=answer.at[th, peer], dst_ref=back.at[th, t_me],
            send_sem=d_send.at[th, slot], recv_sem=d_recv.at[th, T_INV[slot]],
            device_id={"tm": peer}, device_id_type=MESH,
        )

    own_b = [pltpu.make_async_copy(after.at[th, OWN], home.at[th, OWN], own_sem.at[1 + th]) for th in range(2)]
    own_c = [
        [
            pltpu.make_async_copy(grouped.at[th, part, t_me], series.at[th, part, t_me], own_sem.at[3 + 2 * th + part])
            for part in range(2)
        ]
        for th in range(2)
    ]
    own_d = [pltpu.make_async_copy(answer.at[th, t_me], back.at[th, t_me], own_sem.at[7 + th]) for th in range(2)]

    def space_block(th, half):
        base = th * 256 + half * 128

        for pair in range(PAIRS):
            q = q2[pair, :, base:base + 128, :].reshape(256, LANES)
            mix[:, pair * LANES:(pair + 1) * LANES] = attend(q, k[pair], vx[pair], None)
        held = x[half * 8:half * 8 + 8, th * 16:th * 16 + 16, :].reshape(128, WIDTH).astype(F32)
        done = (held + dot(mix[...], ws[3])).astype(BF16)
        after[th, half * 8:half * 8 + 8] = done.reshape(8, 16, WIDTH)
        for slot in B_SENDS[half]:
            if slot == OWN:
                own_b[th].start()
            else:
                b_copy(th, slot).start()

    def regroup(th, part):
        for slot in range(8 * part, 8 * part + 8):
            if slot == OWN:
                own_b[th].wait()
            else:
                pltpu.make_async_remote_copy(
                    src_ref=after.at[th, slot], dst_ref=home.at[th, slot],
                    send_sem=b_send.at[th, slot], recv_sem=b_recv.at[th, slot],
                    device_id={"space": z_peer(s_me, slot)}, device_id_type=MESH,
                ).wait_recv()
        moved = dot(perm[...], home[th, 8 * part:8 * part + 8].reshape(128, WIDTH)).astype(BF16)
        grouped[th, part] = moved.reshape(16, 8, WIDTH)
        own_c[th][part].start()
        for slot in range(15, 0, -1):
            c_copy(th, part, slot).start()

    def time_project(th, part):
        own_c[th][part].wait()
        for slot in range(1, 16):
            pltpu.make_async_remote_copy(
                src_ref=grouped.at[th, part, 0], dst_ref=series.at[th, part, t_peer(t_me, slot)],
                send_sem=c_send.at[th, part, slot], recv_sem=c_recv.at[th, part, slot],
                device_id={"tm": t_peer(t_me, slot)}, device_id_type=MESH,
            ).wait_recv()
        normed = normed_rows(series[th, part].reshape(128, WIDTH))
        for index in range(3):
            made = dot(normed, wt[index])
            for pair in range(PAIRS):
                cols = slice(pair * LANES, (pair + 1) * LANES)
                if index == 0:
                    tq2[pair, 0, part] = (made[:, cols] * first[:, cols]).astype(BF16)
                    tq2[pair, 1, part] = (made[:, cols] * second[:, cols]).astype(BF16)
                elif index == 1:
                    tk[pair, part] = made[:, cols].astype(BF16)
                else:
                    tvx[pair, part, :, :LANES] = made[:, cols].astype(BF16)

    def time_block(th, half):
        rows = 64 * (half + 1)
        bias = (bias0, bias1)[half]
        for pair in range(PAIRS):
            q = tq2[pair, :, :, half * 64:half * 64 + 64, :].reshape(256, LANES)
            keys = tk[pair, :, :rows, :].reshape(2 * rows, LANES)
            values = tvx[pair, :, :rows, :].reshape(2 * rows, 2 * LANES)
            tmix[:, pair * LANES:(pair + 1) * LANES] = attend(q, keys, values, bias[...])
        held = series[th, :, half * 8:half * 8 + 8].reshape(128, WIDTH).astype(F32)
        done = held + dot(tmix[...], wt[3])
        done = jnp.swapaxes(done.reshape(2, 8, 8, WIDTH), 0, 1).reshape(8, 16, WIDTH)
        answer[th, half * 8:half * 8 + 8] = done.astype(BF16)

    def send_answer(th):
        own_d[th].start()
        for slot in range(15, 0, -1):
            d_copy(th, slot).start()

    outs = [
        pltpu.make_async_copy(final.at[th], out.at[:, pl.ds(th * 16, 16), :], out_sem.at[th]) for th in range(2)
    ]

    def finish(th):
        own_d[th].wait()
        for slot in range(1, 16):
            pltpu.make_async_remote_copy(
                src_ref=answer.at[th, 0], dst_ref=back.at[th, t_peer(t_me, slot)],
                send_sem=d_send.at[th, slot], recv_sem=d_recv.at[th, slot],
                device_id={"tm": t_peer(t_me, slot)}, device_id_type=MESH,
            ).wait_recv()
        moved = dot(unperm[...], back[th].reshape(256, WIDTH)).astype(BF16)
        final[th] = moved.reshape(16, 16, WIDTH)
        outs[th].start()

    for th in range(2):
        space_block(th, 0)
        space_block(th, 1)
    regroup(0, 0)
    regroup(0, 1)
    loads[1].wait()
    time_project(0, 0)
    time_project(0, 1)
    regroup(1, 0)
    time_block(0, 0)
    time_block(0, 1)
    regroup(1, 1)
    send_answer(0)
    time_project(1, 0)
    time_project(1, 1)
    time_block(1, 0)
    time_block(1, 1)
    send_answer(1)
    finish(0)
    finish(1)

    for slot in OTHERS:
        a_copy(slot).wait_send()
        for th in range(2):
            b_copy(th, slot).wait_send()
    for slot in range(1, 16):
        for th in range(2):
            for part in range(2):
                c_copy(th, part, slot).wait_send()
            d_copy(th, slot).wait_send()
    for copy in outs:
        copy.wait()


def on_device(clip, w_spatial, w_temporal):
    dma = pltpu.SemaphoreType.DMA
    vmem = pltpu.VMEM
    return pl.pallas_call(
        kernel,
        out_shape=jax.ShapeDtypeStruct(clip.shape, BF16),
        in_specs=[pl.BlockSpec(memory_space=pltpu.HBM)] * 3,
        out_specs=pl.BlockSpec(memory_space=pl.ANY),
        scratch_shapes=[
            vmem((4, WIDTH, WIDTH), BF16),
            vmem((4, WIDTH, WIDTH), BF16),
            vmem((16, 32, WIDTH), BF16),
            vmem((PAIRS, 2, 512, LANES), BF16),
            vmem((PAIRS, 512, LANES), BF16),
            vmem((PAIRS, 512, 2 * LANES), BF16),
            vmem((128, WIDTH), BF16),
            vmem((2, 16, 16, WIDTH), BF16),
            vmem((2, 16, 16, WIDTH), BF16),
            vmem((128, 128), BF16),
            vmem((256, 256), BF16),
            vmem((256, 128), F32),
            vmem((256, 256), F32),
            vmem((2, 2, 16, 8, WIDTH), BF16),
            vmem((2, 2, 16, 8, WIDTH), BF16),
            vmem((PAIRS, 2, 2, 128, LANES), BF16),
            vmem((PAIRS, 2, 128, LANES), BF16),
            vmem((PAIRS, 2, 128, 2 * LANES), BF16),
            vmem((128, WIDTH), BF16),
            vmem((2, 16, 16, WIDTH), BF16),
            vmem((2, 16, 16, WIDTH), BF16),
            vmem((2, 16, 16, WIDTH), BF16),
            dma((2,)),
            dma((16,)), dma((16,)),
            dma((2, 16)), dma((2, 16)),
            dma((2, 2, 16)), dma((2, 2, 16)),
            dma((2, 16)), dma((2, 16)),
            dma((9,)),
            dma((2,)),
        ],
        compiler_params=pltpu.CompilerParams(
            collective_id=0, has_side_effects=True, vmem_limit_bytes=40 * 1024 * 1024
        ),
    )(*(pltpu.with_memory_space_constraint(v, pltpu.HBM) for v in (clip, w_spatial, w_temporal)))


def solution(mesh):
    placed = (P("tm", "space", None), P(), P())
    return jax.shard_map(
        on_device, mesh=mesh, in_specs=placed, out_specs=P("tm", "space", None), check_vma=False
    )
```

```python
import functools
import math

import jax
import jax.numpy as jnp
from jax import lax
from jax.experimental import pallas as pl
from jax.experimental.pallas import tpu as pltpu
from jax.sharding import PartitionSpec as P

MESH = pl.DeviceIdType.MESH
HEAD = 64
LANES = 128
WIDTH = 768
PAIRS = WIDTH // LANES
SCALE = math.log2(math.e) / math.sqrt(HEAD)
BF16 = jnp.bfloat16
F32 = jnp.float32

Z_OFFS = (4, 3, -3, 2, -2, 1, -1, 0)
Z_INV = (0, 2, 1, 4, 3, 6, 5, 7)
HERE = 7
T_OFFS = [(dx, dy) for dx in (0, 1, 3, 2) for dy in (0, 1, 3, 2)]
T_INV = [T_OFFS.index(((-dx) % 4, (-dy) % 4)) for dx, dy in T_OFFS]

Z_GROUPS = ((7, 8), (0, 1), (1, 3), (3, 5), (5, 7))


def z_peer(me, near, core):
    return lax.rem(me // 2 + (Z_OFFS[near] + 8), 8) * 2 + core


def t_peer(me, slot):
    dx, dy = T_OFFS[slot]
    return lax.rem(me // 4 + dx, 4) * 4 + lax.rem(lax.rem(me, 4) + dy, 4)


def normed_rows(rows):
    wide = rows.astype(F32)
    return (wide * lax.rsqrt(jnp.mean(wide * wide, axis=-1, keepdims=True) + 1e-06)).astype(BF16)


def dot(a, b):
    return jnp.dot(a, b, preferred_element_type=F32)


def attend(q, k, vx, bias):
    n = q.shape[0] // 2
    scores = lax.dot_general(q, k, (((1,), (1,)), ((), ())), preferred_element_type=F32)
    if bias is not None:
        scores = scores + bias
    largest = jnp.max(scores, axis=-1, keepdims=True)
    expo = jnp.exp2(scores - largest).astype(BF16)
    both = dot(expo, vx)
    both = both[:, :LANES] / both[:, LANES:]
    lane = lax.broadcasted_iota(jnp.int32, (n, LANES), 1)
    return jnp.where(lane < HEAD, both[:n], both[n:]).astype(BF16)


def kernel(
    clip, w_space, w_time, out,
    ws, wt, x, q2, k, vx, mix, after, home, perm, unperm, bias0, bias1, grouped, series,
    tq2, tk, tvx, tmix, answer, back, final,
    w_sem, a_send, a_recv, b_send, b_recv, c_send, c_recv, d_send, d_recv, own_sem, out_sem,
):
    t_me = lax.axis_index("tm")
    s_me = lax.axis_index("space")
    core = lax.rem(s_me, 2)

    loads = [pltpu.make_async_copy(w_space, ws, w_sem.at[0]), pltpu.make_async_copy(w_time, wt, w_sem.at[1])]
    own_a = pltpu.make_async_copy(clip.at[s_me], x.at[core, HERE], own_sem.at[0])
    own_a.start()
    for load in loads:
        load.start()

    barrier = pltpu.get_barrier_semaphore()
    for near in range(8):
        for dest in (core, 1 - core):
            if near != HERE or dest is not core:
                pl.semaphore_signal(barrier, inc=1, device_id={"space": z_peer(s_me, near, dest)}, device_id_type=MESH)
    for slot in range(15, 0, -1):
        pl.semaphore_signal(barrier, inc=1, device_id={"tm": t_peer(t_me, slot)}, device_id_type=MESH)
    pl.semaphore_wait(barrier, 30)

    def a_copy(near, dest):
        peer = z_peer(s_me, near, dest)
        return pltpu.make_async_remote_copy(
            src_ref=clip.at[peer], dst_ref=x.at[core, Z_INV[near]],
            send_sem=a_send.at[dest, near], recv_sem=a_recv.at[core, Z_INV[near]],
            device_id={"space": peer}, device_id_type=MESH,
        )

    for dest in range(2):
        for near in range(8):
            if near == HERE:
                @pl.when(core != dest)
                def _():
                    a_copy(near, dest).start()
            else:
                a_copy(near, dest).start()

    ones = jnp.ones((512, LANES), BF16)
    for pair in range(PAIRS):
        vx[pair, :, LANES:] = ones
        tvx[pair, :, :, LANES:] = ones[:256].reshape(2, 128, LANES)
    frames = [z_peer(s_me, slot % 8, slot // 8) for slot in range(16)]

    def frame_of(slots):
        found = jnp.zeros_like(slots)
        for slot in range(16):
            found = jnp.where(slots == slot, frames[slot], found)
        return found

    row = lax.broadcasted_iota(jnp.int32, (128, 128), 0)
    col = lax.broadcasted_iota(jnp.int32, (128, 128), 1)
    perm[...] = jnp.where((row // 8 == col % 16) & (row % 8 == col // 16), 1.0, 0.0).astype(BF16)
    row = lax.broadcasted_iota(jnp.int32, (256, 256), 0)
    col = lax.broadcasted_iota(jnp.int32, (1, 256), 1)
    unperm[...] = jnp.where((row // 16 == frame_of(col % 16)) & (row % 16 == col // 16), 1.0, 0.0).astype(BF16)
    for half, bias in enumerate((bias0, bias1)):
        blocks = 8 * (half + 1)
        key = lax.broadcasted_iota(jnp.int32, (1, 16 * blocks), 1)
        key_at = key % (8 * blocks) // 8 * 16 + frame_of(key // (8 * blocks) * 8 + key % 8)
        query = lax.broadcasted_iota(jnp.int32, (256, 1), 0) % 128
        query_at = (query % 64 // 8 + 8 * half) * 16 + frame_of(query // 64 * 8 + query % 8)
        bias[...] = jnp.where(key_at <= query_at, 0.0, -1e30).astype(F32)
    lane = lax.broadcasted_iota(jnp.int32, (1, WIDTH), 1)
    first = jnp.where(lane % LANES < HEAD, SCALE, 0.0).astype(F32)
    second = jnp.where(lane % LANES < HEAD, 0.0, SCALE).astype(F32)

    loads[0].wait()
    own_a.wait()

    def a_wait(near, source):
        pltpu.make_async_remote_copy(
            src_ref=clip.at[0], dst_ref=x.at[source, near],
            send_sem=a_send.at[source, near], recv_sem=a_recv.at[source, near],
            device_id={"space": z_peer(s_me, near, source)}, device_id_type=MESH,
        ).wait_recv()

    for lo, hi in Z_GROUPS:
        for near in range(lo, hi):
            if near == HERE:
                a_wait(near, 1 - core)
            else:
                a_wait(near, 0)
                a_wait(near, 1)
        count = hi - lo
        normed = normed_rows(x[:, lo:hi].reshape(count * 64, WIDTH))
        for index in range(3):
            made = dot(normed, ws[index])
            if index == 0:
                kinds = [((made * first).astype(BF16), q2, 0), ((made * second).astype(BF16), q2, 1)]
            else:
                kinds = [(made.astype(BF16), (k, vx)[index - 1], None)]
            for value, ref, head in kinds:
                value = value.reshape(2, count, 2, 16, WIDTH)
                for th, source in ((0, 0), (0, 1), (1, 0), (1, 1)):
                    part = value[source, :, th].reshape(count * 16, WIDTH)
                    at = pl.ds(th * 256 + source * 128 + lo * 16, count * 16)
                    for pair in range(PAIRS):
                        piece = part[:, pair * LANES:(pair + 1) * LANES]
                        if head is None:
                            ref[pair, at, :LANES] = piece
                        else:
                            ref[pair, head, at, :] = piece

    def b_copy(th, near, dest):
        return pltpu.make_async_remote_copy(
            src_ref=after.at[th, dest, near], dst_ref=home.at[th, core, Z_INV[near]],
            send_sem=b_send.at[th, dest, near], recv_sem=b_recv.at[th, core, Z_INV[near]],
            device_id={"space": z_peer(s_me, near, dest)}, device_id_type=MESH,
        )

    def b_wait(th, near, source):
        pltpu.make_async_remote_copy(
            src_ref=after.at[th, source, near], dst_ref=home.at[th, source, near],
            send_sem=b_send.at[th, source, near], recv_sem=b_recv.at[th, source, near],
            device_id={"space": z_peer(s_me, near, source)}, device_id_type=MESH,
        ).wait_recv()

    def c_copy(th, part, slot):
        peer = t_peer(t_me, slot)
        return pltpu.make_async_remote_copy(
            src_ref=grouped.at[th, part, peer], dst_ref=series.at[th, part, t_me],
            send_sem=c_send.at[th, part, slot], recv_sem=c_recv.at[th, part, T_INV[slot]],
            device_id={"tm": peer}, device_id_type=MESH,
        )

    def d_copy(th, slot):
        peer = t_peer(t_me, slot)
        return pltpu.make_async_remote_copy(
            src_ref=answer.at[th, peer], dst_ref=back.at[th, t_me],
            send_sem=d_send.at[th, slot], recv_sem=d_recv.at[th, T_INV[slot]],
            device_id={"tm": peer}, device_id_type=MESH,
        )

    own_b = [
        pltpu.make_async_copy(after.at[th, core, HERE], home.at[th, core, HERE], own_sem.at[1 + th])
        for th in range(2)
    ]
    own_c = [
        [
            pltpu.make_async_copy(grouped.at[th, part, t_me], series.at[th, part, t_me], own_sem.at[3 + 2 * th + part])
            for part in range(2)
        ]
        for th in range(2)
    ]
    own_d = [pltpu.make_async_copy(answer.at[th, t_me], back.at[th, t_me], own_sem.at[7 + th]) for th in range(2)]

    def space_block(th, half):
        base = th * 256 + half * 128

        for pair in range(PAIRS):
            q = q2[pair, :, base:base + 128, :].reshape(256, LANES)
            mix[:, pair * LANES:(pair + 1) * LANES] = attend(q, k[pair], vx[pair], None)
        held = x[half, :, th * 16:th * 16 + 16, :].reshape(128, WIDTH).astype(F32)
        done = (held + dot(mix[...], ws[3])).astype(BF16)
        after[th, half] = done.reshape(8, 16, WIDTH)
        for near in range(8):
            if near == HERE:
                @pl.when(core == half)
                def _():
                    own_b[th].start()

                @pl.when(core != half)
                def _():
                    b_copy(th, near, half).start()
            else:
                b_copy(th, near, half).start()

    def regroup(th, part):
        for near in range(8):
            if near == HERE:
                @pl.when(core == part)
                def _():
                    own_b[th].wait()

                @pl.when(core != part)
                def _():
                    b_wait(th, near, part)
            else:
                b_wait(th, near, part)
        moved = dot(perm[...], home[th, part].reshape(128, WIDTH)).astype(BF16)
        grouped[th, part] = moved.reshape(16, 8, WIDTH)
        own_c[th][part].start()
        for slot in range(15, 0, -1):
            c_copy(th, part, slot).start()

    def time_project(th, part):
        own_c[th][part].wait()
        for slot in range(1, 16):
            pltpu.make_async_remote_copy(
                src_ref=grouped.at[th, part, 0], dst_ref=series.at[th, part, t_peer(t_me, slot)],
                send_sem=c_send.at[th, part, slot], recv_sem=c_recv.at[th, part, slot],
                device_id={"tm": t_peer(t_me, slot)}, device_id_type=MESH,
            ).wait_recv()
        normed = normed_rows(series[th, part].reshape(128, WIDTH))
        for index in range(3):
            made = dot(normed, wt[index])
            for pair in range(PAIRS):
                cols = slice(pair * LANES, (pair + 1) * LANES)
                if index == 0:
                    tq2[pair, 0, part] = (made[:, cols] * first[:, cols]).astype(BF16)
                    tq2[pair, 1, part] = (made[:, cols] * second[:, cols]).astype(BF16)
                elif index == 1:
                    tk[pair, part] = made[:, cols].astype(BF16)
                else:
                    tvx[pair, part, :, :LANES] = made[:, cols].astype(BF16)

    def time_block(th, half):
        rows = 64 * (half + 1)
        bias = (bias0, bias1)[half]
        for pair in range(PAIRS):
            q = tq2[pair, :, :, half * 64:half * 64 + 64, :].reshape(256, LANES)
            keys = tk[pair, :, :rows, :].reshape(2 * rows, LANES)
            values = tvx[pair, :, :rows, :].reshape(2 * rows, 2 * LANES)
            tmix[:, pair * LANES:(pair + 1) * LANES] = attend(q, keys, values, bias[...])
        held = series[th, :, half * 8:half * 8 + 8].reshape(128, WIDTH).astype(F32)
        done = held + dot(tmix[...], wt[3])
        done = jnp.swapaxes(done.reshape(2, 8, 8, WIDTH), 0, 1).reshape(8, 16, WIDTH)
        answer[th, half * 8:half * 8 + 8] = done.astype(BF16)

    def send_answer(th):
        own_d[th].start()
        for slot in range(15, 0, -1):
            d_copy(th, slot).start()

    outs = [
        pltpu.make_async_copy(final.at[th], out.at[:, pl.ds(th * 16, 16), :], out_sem.at[th]) for th in range(2)
    ]

    def finish(th):
        own_d[th].wait()
        for slot in range(1, 16):
            pltpu.make_async_remote_copy(
                src_ref=answer.at[th, 0], dst_ref=back.at[th, t_peer(t_me, slot)],
                send_sem=d_send.at[th, slot], recv_sem=d_recv.at[th, slot],
                device_id={"tm": t_peer(t_me, slot)}, device_id_type=MESH,
            ).wait_recv()
        moved = dot(unperm[...], back[th].reshape(256, WIDTH)).astype(BF16)
        final[th] = moved.reshape(16, 16, WIDTH)
        outs[th].start()

    for th in range(2):
        space_block(th, 0)
        space_block(th, 1)
    loads[1].wait()
    regroup(0, 0)
    time_project(0, 0)
    regroup(0, 1)
    regroup(1, 0)
    time_project(0, 1)
    regroup(1, 1)
    time_block(0, 0)
    time_block(0, 1)
    send_answer(0)
    time_project(1, 0)
    time_project(1, 1)
    time_block(1, 0)
    time_block(1, 1)
    send_answer(1)
    finish(0)
    finish(1)

    for near in range(8):
        for dest in (core, 1 - core):
            if near != HERE or dest is not core:
                a_copy(near, dest).wait_send()
                b_copy(0, near, dest).wait_send()
                b_copy(1, near, dest).wait_send()
    for slot in range(1, 16):
        for th in range(2):
            for part in range(2):
                c_copy(th, part, slot).wait_send()
            d_copy(th, slot).wait_send()
    for copy in outs:
        copy.wait()


def on_device(clip, w_spatial, w_temporal):
    dma = pltpu.SemaphoreType.DMA
    vmem = pltpu.VMEM
    return pl.pallas_call(
        kernel,
        out_shape=jax.ShapeDtypeStruct(clip.shape, BF16),
        in_specs=[pl.BlockSpec(memory_space=pltpu.HBM)] * 3,
        out_specs=pl.BlockSpec(memory_space=pl.ANY),
        scratch_shapes=[
            vmem((4, WIDTH, WIDTH), BF16),
            vmem((4, WIDTH, WIDTH), BF16),
            vmem((2, 8, 32, WIDTH), BF16),
            vmem((PAIRS, 2, 512, LANES), BF16),
            vmem((PAIRS, 512, LANES), BF16),
            vmem((PAIRS, 512, 2 * LANES), BF16),
            vmem((128, WIDTH), BF16),
            vmem((2, 2, 8, 16, WIDTH), BF16),
            vmem((2, 2, 8, 16, WIDTH), BF16),
            vmem((128, 128), BF16),
            vmem((256, 256), BF16),
            vmem((256, 128), F32),
            vmem((256, 256), F32),
            vmem((2, 2, 16, 8, WIDTH), BF16),
            vmem((2, 2, 16, 8, WIDTH), BF16),
            vmem((PAIRS, 2, 2, 128, LANES), BF16),
            vmem((PAIRS, 2, 128, LANES), BF16),
            vmem((PAIRS, 2, 128, 2 * LANES), BF16),
            vmem((128, WIDTH), BF16),
            vmem((2, 16, 16, WIDTH), BF16),
            vmem((2, 16, 16, WIDTH), BF16),
            vmem((2, 16, 16, WIDTH), BF16),
            dma((2,)),
            dma((2, 8)), dma((2, 8)),
            dma((2, 2, 8)), dma((2, 2, 8)),
            dma((2, 2, 16)), dma((2, 2, 16)),
            dma((2, 16)), dma((2, 16)),
            dma((9,)),
            dma((2,)),
        ],
        compiler_params=pltpu.CompilerParams(
            collective_id=0, has_side_effects=True, vmem_limit_bytes=40 * 1024 * 1024
        ),
    )(*(pltpu.with_memory_space_constraint(v, pltpu.HBM) for v in (clip, w_spatial, w_temporal)))


def solution(mesh):
    placed = (P("tm", "space", None), P(), P())
    return jax.shard_map(
        on_device, mesh=mesh, in_specs=placed, out_specs=P("tm", "space", None), check_vma=False
    )
```

```python
import functools
import math

import jax
import jax.numpy as jnp
from jax import lax
from jax.experimental import pallas as pl
from jax.experimental.pallas import tpu as pltpu
from jax.sharding import PartitionSpec as P

MESH = pl.DeviceIdType.MESH
HEAD = 64
LANES = 128
WIDTH = 768
PAIRS = WIDTH // LANES
SCALE = math.log2(math.e) / math.sqrt(HEAD)
BF16 = jnp.bfloat16
F32 = jnp.float32

Z_OFFS = (4, 3, -3, 2, -2, 1, -1, 0)
Z_INV = (0, 2, 1, 4, 3, 6, 5, 7)
HERE = 7
T_OFFS = [(dx, dy) for dx in (0, 1, 3, 2) for dy in (0, 1, 3, 2)]
Y_STEPS = tuple(T_OFFS.index((0, dy)) for dy in (1, 3, 2))
X_STEPS = tuple(T_OFFS.index((dx, 0)) for dx in (1, 3, 2))
T_INV = [T_OFFS.index(((-dx) % 4, (-dy) % 4)) for dx, dy in T_OFFS]

Z_GROUPS = ((7, 8), (0, 1), (1, 3), (3, 5), (5, 7))


def z_peer(me, near, core):
    return lax.rem(me // 2 + (Z_OFFS[near] + 8), 8) * 2 + core


def t_peer(me, slot):
    dx, dy = T_OFFS[slot]
    return lax.rem(me // 4 + dx, 4) * 4 + lax.rem(lax.rem(me, 4) + dy, 4)


def normed_rows(rows):
    wide = rows.astype(F32)
    return (wide * lax.rsqrt(jnp.mean(wide * wide, axis=-1, keepdims=True) + 1e-06)).astype(BF16)


def dot(a, b):
    return jnp.dot(a, b, preferred_element_type=F32)


def attend(q, k, vx, bias):
    n = q.shape[0] // 2
    scores = lax.dot_general(q, k, (((1,), (1,)), ((), ())), preferred_element_type=F32)
    if bias is not None:
        scores = scores + bias
    largest = jnp.max(scores, axis=-1, keepdims=True)
    expo = jnp.exp2(scores - largest).astype(BF16)
    both = dot(expo, vx)
    both = both[:, :LANES] / both[:, LANES:]
    lane = lax.broadcasted_iota(jnp.int32, (n, LANES), 1)
    return jnp.where(lane < HEAD, both[:n], both[n:]).astype(BF16)


def kernel(
    clip, w_space, w_time, out,
    ws, wt, x, q2, k, vx, mix, after, home, perm, unperm, bias0, bias1, grouped, series,
    tq2, tk, tvx, tmix, answer, back,
    w_sem, a_send, a_recv, b_send, b_recv, c_send, c_recv, d_send, d_recv, own_sem, y_sem, x_sem, all_sem,
):
    t_me = lax.axis_index("tm")
    s_me = lax.axis_index("space")
    core = lax.rem(s_me, 2)

    loads = [pltpu.make_async_copy(w_space, ws, w_sem.at[0]), pltpu.make_async_copy(w_time, wt, w_sem.at[1])]
    own_a = pltpu.make_async_copy(clip.at[s_me], x.at[core, HERE], own_sem.at[0])
    own_a.start()
    for load in loads:
        load.start()

    barrier = pltpu.get_barrier_semaphore()
    for near in range(8):
        for dest in (core, 1 - core):
            if near != HERE or dest is not core:
                pl.semaphore_signal(barrier, inc=1, device_id={"space": z_peer(s_me, near, dest)}, device_id_type=MESH)
    for slot in (Y_STEPS[0], Y_STEPS[1], X_STEPS[0], X_STEPS[1]):
        pl.semaphore_signal(barrier, inc=1, device_id={"tm": t_peer(t_me, slot)}, device_id_type=MESH)
    pl.semaphore_wait(barrier, 19)
    for slot in Y_STEPS[:2]:
        pl.semaphore_signal(y_sem, inc=1, device_id={"tm": t_peer(t_me, slot)}, device_id_type=MESH)
    for slot in X_STEPS[:2]:
        pl.semaphore_signal(x_sem, inc=1, device_id={"tm": t_peer(t_me, slot)}, device_id_type=MESH)

    def a_copy(near, dest):
        peer = z_peer(s_me, near, dest)
        return pltpu.make_async_remote_copy(
            src_ref=clip.at[peer], dst_ref=x.at[core, Z_INV[near]],
            send_sem=a_send.at[dest, near], recv_sem=a_recv.at[core, Z_INV[near]],
            device_id={"space": peer}, device_id_type=MESH,
        )

    for dest in range(2):
        for near in range(8):
            if near == HERE:
                @pl.when(core != dest)
                def _():
                    a_copy(near, dest).start()
            else:
                a_copy(near, dest).start()

    ones = jnp.ones((512, LANES), BF16)
    for pair in range(PAIRS):
        vx[pair, :, LANES:] = ones
        tvx[pair, :, :, LANES:] = ones[:256].reshape(2, 128, LANES)
    frames = [z_peer(s_me, slot % 8, slot // 8) for slot in range(16)]

    def frame_of(slots):
        found = jnp.zeros_like(slots)
        for slot in range(16):
            found = jnp.where(slots == slot, frames[slot], found)
        return found

    row = lax.broadcasted_iota(jnp.int32, (128, 128), 0)
    col = lax.broadcasted_iota(jnp.int32, (128, 128), 1)
    perm[...] = jnp.where((row // 8 == col % 16) & (row % 8 == col // 16), 1.0, 0.0).astype(BF16)
    row = lax.broadcasted_iota(jnp.int32, (256, 256), 0)
    col = lax.broadcasted_iota(jnp.int32, (1, 256), 1)
    unperm[...] = jnp.where((row // 16 == frame_of(col % 16)) & (row % 16 == col // 16), 1.0, 0.0).astype(BF16)
    for half, bias in enumerate((bias0, bias1)):
        blocks = 8 * (half + 1)
        key = lax.broadcasted_iota(jnp.int32, (1, 16 * blocks), 1)
        key_at = key % (8 * blocks) // 8 * 16 + frame_of(key // (8 * blocks) * 8 + key % 8)
        query = lax.broadcasted_iota(jnp.int32, (256, 1), 0) % 128
        query_at = (query % 64 // 8 + 8 * half) * 16 + frame_of(query // 64 * 8 + query % 8)
        bias[...] = jnp.where(key_at <= query_at, 0.0, -1e30).astype(F32)
    lane = lax.broadcasted_iota(jnp.int32, (1, WIDTH), 1)
    first = jnp.where(lane % LANES < HEAD, SCALE, 0.0).astype(F32)
    second = jnp.where(lane % LANES < HEAD, 0.0, SCALE).astype(F32)

    loads[0].wait()
    own_a.wait()

    def a_wait(near, source):
        pltpu.make_async_remote_copy(
            src_ref=clip.at[0], dst_ref=x.at[source, near],
            send_sem=a_send.at[source, near], recv_sem=a_recv.at[source, near],
            device_id={"space": z_peer(s_me, near, source)}, device_id_type=MESH,
        ).wait_recv()

    for lo, hi in Z_GROUPS:
        for near in range(lo, hi):
            if near == HERE:
                a_wait(near, 1 - core)
            else:
                a_wait(near, 0)
                a_wait(near, 1)
        count = hi - lo
        normed = normed_rows(x[:, lo:hi].reshape(count * 64, WIDTH))
        for index in range(3):
            made = dot(normed, ws[index])
            if index == 0:
                kinds = [((made * first).astype(BF16), q2, 0), ((made * second).astype(BF16), q2, 1)]
            else:
                kinds = [(made.astype(BF16), (k, vx)[index - 1], None)]
            for value, ref, head in kinds:
                value = value.reshape(2, count, 2, 16, WIDTH)
                for th, source in ((0, 0), (0, 1), (1, 0), (1, 1)):
                    part = value[source, :, th].reshape(count * 16, WIDTH)
                    at = pl.ds(th * 256 + source * 128 + lo * 16, count * 16)
                    for pair in range(PAIRS):
                        piece = part[:, pair * LANES:(pair + 1) * LANES]
                        if head is None:
                            ref[pair, at, :LANES] = piece
                        else:
                            ref[pair, head, at, :] = piece

    def b_copy(th, near, dest):
        return pltpu.make_async_remote_copy(
            src_ref=after.at[th, dest, near], dst_ref=home.at[th, core, Z_INV[near]],
            send_sem=b_send.at[th, dest, near], recv_sem=b_recv.at[th, core, Z_INV[near]],
            device_id={"space": z_peer(s_me, near, dest)}, device_id_type=MESH,
        )

    def b_wait(th, near, source):
        pltpu.make_async_remote_copy(
            src_ref=after.at[th, source, near], dst_ref=home.at[th, source, near],
            send_sem=b_send.at[th, source, near], recv_sem=b_recv.at[th, source, near],
            device_id={"space": z_peer(s_me, near, source)}, device_id_type=MESH,
        ).wait_recv()

    def c_copy(th, part, slot):
        peer = t_peer(t_me, slot)
        return pltpu.make_async_remote_copy(
            src_ref=grouped.at[th, part, peer], dst_ref=series.at[th, part, t_me],
            send_sem=c_send.at[th, part, slot], recv_sem=c_recv.at[th, part, T_INV[slot]],
            device_id={"tm": peer}, device_id_type=MESH,
        )

    def d_copy(th, slot):
        peer = t_peer(t_me, slot)
        return pltpu.make_async_remote_copy(
            src_ref=answer.at[th, peer], dst_ref=back.at[th, t_me],
            send_sem=d_send.at[th, slot], recv_sem=d_recv.at[th, T_INV[slot]],
            device_id={"tm": peer}, device_id_type=MESH,
        )

    own_b = [
        pltpu.make_async_copy(after.at[th, core, HERE], home.at[th, core, HERE], own_sem.at[1 + th])
        for th in range(2)
    ]
    own_c = [
        [
            pltpu.make_async_copy(grouped.at[th, part, t_me], series.at[th, part, t_me], own_sem.at[3 + 2 * th + part])
            for part in range(2)
        ]
        for th in range(2)
    ]
    own_d = [pltpu.make_async_copy(answer.at[th, t_me], back.at[th, t_me], own_sem.at[7 + th]) for th in range(2)]

    def space_block(th, half):
        base = th * 256 + half * 128

        for pair in range(PAIRS):
            q = q2[pair, :, base:base + 128, :].reshape(256, LANES)
            mix[:, pair * LANES:(pair + 1) * LANES] = attend(q, k[pair], vx[pair], None)
        held = x[half, :, th * 16:th * 16 + 16, :].reshape(128, WIDTH).astype(F32)
        done = (held + dot(mix[...], ws[3])).astype(BF16)
        after[th, half] = done.reshape(8, 16, WIDTH)
        for near in range(8):
            if near == HERE:
                @pl.when(core == half)
                def _():
                    own_b[th].start()

                @pl.when(core != half)
                def _():
                    b_copy(th, near, half).start()
            else:
                b_copy(th, near, half).start()

    def regroup(th, part):
        for near in range(8):
            if near == HERE:
                @pl.when(core == part)
                def _():
                    own_b[th].wait()

                @pl.when(core != part)
                def _():
                    b_wait(th, near, part)
            else:
                b_wait(th, near, part)
        moved = dot(perm[...], home[th, part].reshape(128, WIDTH)).astype(BF16)
        grouped[th, part] = moved.reshape(16, 8, WIDTH)
        own_c[th][part].start()
        for slot in range(15, 0, -1):
            c_copy(th, part, slot).start()

    def time_project(th, part):
        own_c[th][part].wait()
        for slot in range(1, 16):
            pltpu.make_async_remote_copy(
                src_ref=grouped.at[th, part, 0], dst_ref=series.at[th, part, t_peer(t_me, slot)],
                send_sem=c_send.at[th, part, slot], recv_sem=c_recv.at[th, part, slot],
                device_id={"tm": t_peer(t_me, slot)}, device_id_type=MESH,
            ).wait_recv()
        normed = normed_rows(series[th, part].reshape(128, WIDTH))
        for index in range(3):
            made = dot(normed, wt[index])
            for pair in range(PAIRS):
                cols = slice(pair * LANES, (pair + 1) * LANES)
                if index == 0:
                    tq2[pair, 0, part] = (made[:, cols] * first[:, cols]).astype(BF16)
                    tq2[pair, 1, part] = (made[:, cols] * second[:, cols]).astype(BF16)
                elif index == 1:
                    tk[pair, part] = made[:, cols].astype(BF16)
                else:
                    tvx[pair, part, :, :LANES] = made[:, cols].astype(BF16)

    def time_block(th, half):
        rows = 64 * (half + 1)
        bias = (bias0, bias1)[half]
        for pair in range(PAIRS):
            q = tq2[pair, :, :, half * 64:half * 64 + 64, :].reshape(256, LANES)
            keys = tk[pair, :, :rows, :].reshape(2 * rows, LANES)
            values = tvx[pair, :, :rows, :].reshape(2 * rows, 2 * LANES)
            tmix[:, pair * LANES:(pair + 1) * LANES] = attend(q, keys, values, bias[...])
        held = series[th, :, half * 8:half * 8 + 8].reshape(128, WIDTH).astype(F32)
        done = held + dot(tmix[...], wt[3])
        done = jnp.swapaxes(done.reshape(2, 8, 8, WIDTH), 0, 1).reshape(8, 16, WIDTH)
        answer[th, half * 8:half * 8 + 8] = done.astype(BF16)

    def send_answer(th):
        own_d[th].start()
        for slot in range(15, 0, -1):
            d_copy(th, slot).start()

    def finish(th):
        own_d[th].wait()
        for slot in range(1, 16):
            pltpu.make_async_remote_copy(
                src_ref=answer.at[th, 0], dst_ref=back.at[th, t_peer(t_me, slot)],
                send_sem=d_send.at[th, slot], recv_sem=d_recv.at[th, slot],
                device_id={"tm": t_peer(t_me, slot)}, device_id_type=MESH,
            ).wait_recv()
        moved = dot(unperm[...], back[th].reshape(256, WIDTH)).astype(BF16)
        out[:, th * 16:th * 16 + 16, :] = moved.reshape(16, 16, WIDTH)

    pl.semaphore_wait(y_sem, 2)
    pl.semaphore_wait(x_sem, 2)
    for slot in Y_STEPS:
        pl.semaphore_signal(all_sem, inc=1, device_id={"tm": t_peer(t_me, slot)}, device_id_type=MESH)
    for th in range(2):
        space_block(th, 0)
        space_block(th, 1)
    loads[1].wait()
    pl.semaphore_wait(all_sem, 3)
    regroup(0, 0)
    time_project(0, 0)
    regroup(0, 1)
    regroup(1, 0)
    time_project(0, 1)
    regroup(1, 1)
    time_block(0, 0)
    time_block(0, 1)
    send_answer(0)
    time_project(1, 0)
    time_project(1, 1)
    time_block(1, 0)
    time_block(1, 1)
    send_answer(1)
    finish(0)
    finish(1)

    for near in range(8):
        for dest in (core, 1 - core):
            if near != HERE or dest is not core:
                a_copy(near, dest).wait_send()
                b_copy(0, near, dest).wait_send()
                b_copy(1, near, dest).wait_send()
    for slot in range(1, 16):
        for th in range(2):
            for part in range(2):
                c_copy(th, part, slot).wait_send()
            d_copy(th, slot).wait_send()


def on_device(clip, w_spatial, w_temporal):
    dma = pltpu.SemaphoreType.DMA
    vmem = pltpu.VMEM
    return pl.pallas_call(
        kernel,
        out_shape=jax.ShapeDtypeStruct(clip.shape, BF16),
        in_specs=[pl.BlockSpec(memory_space=pltpu.HBM)] * 3,
        out_specs=pl.BlockSpec(memory_space=pltpu.VMEM),
        scratch_shapes=[
            vmem((4, WIDTH, WIDTH), BF16),
            vmem((4, WIDTH, WIDTH), BF16),
            vmem((2, 8, 32, WIDTH), BF16),
            vmem((PAIRS, 2, 512, LANES), BF16),
            vmem((PAIRS, 512, LANES), BF16),
            vmem((PAIRS, 512, 2 * LANES), BF16),
            vmem((128, WIDTH), BF16),
            vmem((2, 2, 8, 16, WIDTH), BF16),
            vmem((2, 2, 8, 16, WIDTH), BF16),
            vmem((128, 128), BF16),
            vmem((256, 256), BF16),
            vmem((256, 128), F32),
            vmem((256, 256), F32),
            vmem((2, 2, 16, 8, WIDTH), BF16),
            vmem((2, 2, 16, 8, WIDTH), BF16),
            vmem((PAIRS, 2, 2, 128, LANES), BF16),
            vmem((PAIRS, 2, 128, LANES), BF16),
            vmem((PAIRS, 2, 128, 2 * LANES), BF16),
            vmem((128, WIDTH), BF16),
            vmem((2, 16, 16, WIDTH), BF16),
            vmem((2, 16, 16, WIDTH), BF16),
            dma((2,)),
            dma((2, 8)), dma((2, 8)),
            dma((2, 2, 8)), dma((2, 2, 8)),
            dma((2, 2, 16)), dma((2, 2, 16)),
            dma((2, 16)), dma((2, 16)),
            dma((9,)),
            pltpu.SemaphoreType.REGULAR,
            pltpu.SemaphoreType.REGULAR,
            pltpu.SemaphoreType.REGULAR,
        ],
        compiler_params=pltpu.CompilerParams(
            collective_id=0, has_side_effects=True, vmem_limit_bytes=40 * 1024 * 1024
        ),
    )(*(pltpu.with_memory_space_constraint(v, pltpu.HBM) for v in (clip, w_spatial, w_temporal)))


def solution(mesh):
    placed = (P("tm", "space", None), P(), P())
    return jax.shard_map(
        on_device, mesh=mesh, in_specs=placed, out_specs=P("tm", "space", None), check_vma=False
    )
```

```python
import functools
import math

import jax
import jax.numpy as jnp
from jax import lax
from jax.experimental import pallas as pl
from jax.experimental.pallas import tpu as pltpu
from jax.sharding import PartitionSpec as P

MESH = pl.DeviceIdType.MESH
HEAD = 64
LANES = 128
WIDTH = 768
PAIRS = WIDTH // LANES
SCALE = math.log2(math.e) / math.sqrt(HEAD)
BF16 = jnp.bfloat16
F32 = jnp.float32

Z_OFFS = (4, 3, -3, 2, -2, 1, -1, 0)
Z_INV = (0, 2, 1, 4, 3, 6, 5, 7)
HERE = 7
T_OFFS = [(dx, dy) for dx in (0, 1, 3, 2) for dy in (0, 1, 3, 2)]
Y_STEPS = tuple(T_OFFS.index((0, dy)) for dy in (1, 3, 2))
X_STEPS = tuple(T_OFFS.index((dx, 0)) for dx in (1, 3, 2))
T_INV = [T_OFFS.index(((-dx) % 4, (-dy) % 4)) for dx, dy in T_OFFS]

Z_GROUPS = ((7, 8), (0, 1), (1, 3), (3, 5), (5, 7))


def z_peer(me, near, core):
    return lax.rem(me // 2 + (Z_OFFS[near] + 8), 8) * 2 + core


def t_peer(me, slot):
    dx, dy = T_OFFS[slot]
    return lax.rem(me // 4 + dx, 4) * 4 + lax.rem(lax.rem(me, 4) + dy, 4)


def normed_rows(rows):
    wide = rows.astype(F32)
    return (wide * lax.rsqrt(jnp.mean(wide * wide, axis=-1, keepdims=True) + 1e-06)).astype(BF16)


def dot(a, b):
    return jnp.dot(a, b, preferred_element_type=F32)


def attend(q, k, vx, bias):
    n = q.shape[0] // 2
    scores = lax.dot_general(q, k, (((1,), (1,)), ((), ())), preferred_element_type=F32)
    if bias is not None:
        scores = scores + bias
    largest = jnp.max(scores, axis=-1, keepdims=True)
    expo = jnp.exp2(scores - largest).astype(BF16)
    both = dot(expo, vx)
    both = both[:, :LANES] / both[:, LANES:]
    lane = lax.broadcasted_iota(jnp.int32, (n, LANES), 1)
    return jnp.where(lane < HEAD, both[:n], both[n:]).astype(BF16)


def kernel(
    clip, w_space, w_time, out,
    ws, wt, x, q2, k, vx, mix, after, home, perm, unperm, bias0, bias1, grouped, series,
    tq2, tk, tvx, tmix, answer, back,
    w_sem, a_send, a_recv, b_send, b_recv, c_send, c_recv, d_send, d_recv, own_sem, y_sem, x_sem, all_sem,
):
    t_me = lax.axis_index("tm")
    s_me = lax.axis_index("space")
    core = lax.rem(s_me, 2)

    loads = [pltpu.make_async_copy(w_space, ws, w_sem.at[0]), pltpu.make_async_copy(w_time, wt, w_sem.at[1])]
    own_a = pltpu.make_async_copy(clip.at[s_me], x.at[core, HERE], own_sem.at[0])
    own_a.start()
    for load in loads:
        load.start()

    barrier = pltpu.get_barrier_semaphore()
    for near in range(8):
        for dest in (core, 1 - core):
            if near != HERE or dest is not core:
                pl.semaphore_signal(barrier, inc=1, device_id={"space": z_peer(s_me, near, dest)}, device_id_type=MESH)
    for slot in (Y_STEPS[0], Y_STEPS[1], X_STEPS[0], X_STEPS[1]):
        pl.semaphore_signal(barrier, inc=1, device_id={"tm": t_peer(t_me, slot)}, device_id_type=MESH)
    pl.semaphore_wait(barrier, 19)
    for slot in Y_STEPS[:2]:
        pl.semaphore_signal(y_sem, inc=1, device_id={"tm": t_peer(t_me, slot)}, device_id_type=MESH)
    for slot in X_STEPS[:2]:
        pl.semaphore_signal(x_sem, inc=1, device_id={"tm": t_peer(t_me, slot)}, device_id_type=MESH)

    def a_copy(near, dest):
        peer = z_peer(s_me, near, dest)
        return pltpu.make_async_remote_copy(
            src_ref=clip.at[peer], dst_ref=x.at[core, Z_INV[near]],
            send_sem=a_send.at[dest, near], recv_sem=a_recv.at[core, Z_INV[near]],
            device_id={"space": peer}, device_id_type=MESH,
        )

    for dest in range(2):
        for near in range(8):
            if near == HERE:
                @pl.when(core != dest)
                def _():
                    a_copy(near, dest).start()
            else:
                a_copy(near, dest).start()

    ones = jnp.ones((512, LANES), BF16)
    for pair in range(PAIRS):
        vx[pair, :, LANES:] = ones
        tvx[pair, :, :, LANES:] = ones[:256].reshape(2, 128, LANES)
    frames = [z_peer(s_me, slot % 8, slot // 8) for slot in range(16)]

    def frame_of(slots):
        found = jnp.zeros_like(slots)
        for slot in range(16):
            found = jnp.where(slots == slot, frames[slot], found)
        return found

    row = lax.broadcasted_iota(jnp.int32, (128, 128), 0)
    col = lax.broadcasted_iota(jnp.int32, (128, 128), 1)
    perm[...] = jnp.where((row // 8 == col % 16) & (row % 8 == col // 16), 1.0, 0.0).astype(BF16)
    row = lax.broadcasted_iota(jnp.int32, (256, 256), 0)
    col = lax.broadcasted_iota(jnp.int32, (1, 256), 1)
    unperm[...] = jnp.where((row // 16 == frame_of(col % 16)) & (row % 16 == col // 16), 1.0, 0.0).astype(BF16)
    for half, bias in enumerate((bias0, bias1)):
        blocks = 8 * (half + 1)
        key = lax.broadcasted_iota(jnp.int32, (1, 16 * blocks), 1)
        key_at = key % (8 * blocks) // 8 * 16 + frame_of(key // (8 * blocks) * 8 + key % 8)
        query = lax.broadcasted_iota(jnp.int32, (256, 1), 0) % 128
        query_at = (query % 64 // 8 + 8 * half) * 16 + frame_of(query // 64 * 8 + query % 8)
        bias[...] = jnp.where(key_at <= query_at, 0.0, -1e30).astype(F32)
    lane = lax.broadcasted_iota(jnp.int32, (1, WIDTH), 1)
    first = jnp.where(lane % LANES < HEAD, SCALE, 0.0).astype(F32)
    second = jnp.where(lane % LANES < HEAD, 0.0, SCALE).astype(F32)

    loads[0].wait()
    own_a.wait()

    def a_wait(near, source):
        pltpu.make_async_remote_copy(
            src_ref=clip.at[0], dst_ref=x.at[source, near],
            send_sem=a_send.at[source, near], recv_sem=a_recv.at[source, near],
            device_id={"space": z_peer(s_me, near, source)}, device_id_type=MESH,
        ).wait_recv()

    for lo, hi in Z_GROUPS:
        for near in range(lo, hi):
            if near == HERE:
                a_wait(near, 1 - core)
            else:
                a_wait(near, 0)
                a_wait(near, 1)
        count = hi - lo
        normed = normed_rows(x[:, lo:hi].reshape(count * 64, WIDTH))
        for index in range(3):
            made = dot(normed, ws[index])
            if index == 0:
                kinds = [((made * first).astype(BF16), q2, 0), ((made * second).astype(BF16), q2, 1)]
            else:
                kinds = [(made.astype(BF16), (k, vx)[index - 1], None)]
            for value, ref, head in kinds:
                value = value.reshape(2, count, 2, 16, WIDTH)
                for th, source in ((0, 0), (0, 1), (1, 0), (1, 1)):
                    part = value[source, :, th].reshape(count * 16, WIDTH)
                    at = pl.ds(th * 256 + source * 128 + lo * 16, count * 16)
                    for pair in range(PAIRS):
                        piece = part[:, pair * LANES:(pair + 1) * LANES]
                        if head is None:
                            ref[pair, at, :LANES] = piece
                        else:
                            ref[pair, head, at, :] = piece

    def b_copy(th, near, dest):
        return pltpu.make_async_remote_copy(
            src_ref=after.at[th, dest, near], dst_ref=home.at[th, core, Z_INV[near]],
            send_sem=b_send.at[th, dest, near], recv_sem=b_recv.at[th, core, Z_INV[near]],
            device_id={"space": z_peer(s_me, near, dest)}, device_id_type=MESH,
        )

    def b_wait(th, near, source):
        pltpu.make_async_remote_copy(
            src_ref=after.at[th, source, near], dst_ref=home.at[th, source, near],
            send_sem=b_send.at[th, source, near], recv_sem=b_recv.at[th, source, near],
            device_id={"space": z_peer(s_me, near, source)}, device_id_type=MESH,
        ).wait_recv()

    def c_copy(th, part, slot):
        peer = t_peer(t_me, slot)
        return pltpu.make_async_remote_copy(
            src_ref=grouped.at[th, part, peer], dst_ref=series.at[th, part, t_me],
            send_sem=c_send.at[th, part, slot], recv_sem=c_recv.at[th, part, T_INV[slot]],
            device_id={"tm": peer}, device_id_type=MESH,
        )

    def d_copy(th, slot):
        peer = t_peer(t_me, slot)
        return pltpu.make_async_remote_copy(
            src_ref=answer.at[th, peer], dst_ref=back.at[th, t_me],
            send_sem=d_send.at[th, slot], recv_sem=d_recv.at[th, T_INV[slot]],
            device_id={"tm": peer}, device_id_type=MESH,
        )

    own_b = [
        pltpu.make_async_copy(after.at[th, core, HERE], home.at[th, core, HERE], own_sem.at[1 + th])
        for th in range(2)
    ]
    own_c = [
        [
            pltpu.make_async_copy(grouped.at[th, part, t_me], series.at[th, part, t_me], own_sem.at[3 + 2 * th + part])
            for part in range(2)
        ]
        for th in range(2)
    ]
    own_d = [pltpu.make_async_copy(answer.at[th, t_me], back.at[th, t_me], own_sem.at[7 + th]) for th in range(2)]

    def space_block(th, half):
        base = th * 256 + half * 128

        for pair in range(PAIRS):
            q = q2[pair, :, base:base + 128, :].reshape(256, LANES)
            mix[:, pair * LANES:(pair + 1) * LANES] = attend(q, k[pair], vx[pair], None)
        held = x[half, :, th * 16:th * 16 + 16, :].reshape(128, WIDTH).astype(F32)
        done = (held + dot(mix[...], ws[3])).astype(BF16)
        after[th, half] = done.reshape(8, 16, WIDTH)
        for near in range(8):
            if near == HERE:
                @pl.when(core == half)
                def _():
                    own_b[th].start()

                @pl.when(core != half)
                def _():
                    b_copy(th, near, half).start()
            else:
                b_copy(th, near, half).start()

    def regroup(th, part):
        for near in range(8):
            if near == HERE:
                @pl.when(core == part)
                def _():
                    own_b[th].wait()

                @pl.when(core != part)
                def _():
                    b_wait(th, near, part)
            else:
                b_wait(th, near, part)
        moved = dot(perm[...], home[th, part].reshape(128, WIDTH)).astype(BF16)
        grouped[th, part] = moved.reshape(16, 8, WIDTH)
        own_c[th][part].start()
        for slot in range(15, 0, -1):
            c_copy(th, part, slot).start()

    def time_project(th, part):
        own_c[th][part].wait()
        for slot in range(1, 16):
            pltpu.make_async_remote_copy(
                src_ref=grouped.at[th, part, 0], dst_ref=series.at[th, part, t_peer(t_me, slot)],
                send_sem=c_send.at[th, part, slot], recv_sem=c_recv.at[th, part, slot],
                device_id={"tm": t_peer(t_me, slot)}, device_id_type=MESH,
            ).wait_recv()
        normed = normed_rows(series[th, part].reshape(128, WIDTH))
        for index in range(3):
            made = dot(normed, wt[index])
            for pair in range(PAIRS):
                cols = slice(pair * LANES, (pair + 1) * LANES)
                if index == 0:
                    tq2[pair, 0, part] = (made[:, cols] * first[:, cols]).astype(BF16)
                    tq2[pair, 1, part] = (made[:, cols] * second[:, cols]).astype(BF16)
                elif index == 1:
                    tk[pair, part] = made[:, cols].astype(BF16)
                else:
                    tvx[pair, part, :, :LANES] = made[:, cols].astype(BF16)

    def time_block(th, half):
        rows = 64 * (half + 1)
        bias = (bias0, bias1)[half]
        for pair in range(PAIRS):
            q = tq2[pair, :, :, half * 64:half * 64 + 64, :].reshape(256, LANES)
            keys = tk[pair, :, :rows, :].reshape(2 * rows, LANES)
            values = tvx[pair, :, :rows, :].reshape(2 * rows, 2 * LANES)
            tmix[half * 128:half * 128 + 128, pair * LANES:(pair + 1) * LANES] = attend(q, keys, values, bias[...])

    def send_answer(th):
        made = dot(tmix[...], wt[3])
        for half in range(2):
            held = series[th, :, half * 8:half * 8 + 8].reshape(128, WIDTH).astype(F32)
            done = held + made[half * 128:half * 128 + 128]
            done = jnp.swapaxes(done.reshape(2, 8, 8, WIDTH), 0, 1).reshape(8, 16, WIDTH)
            answer[th, half * 8:half * 8 + 8] = done.astype(BF16)
        own_d[th].start()
        for slot in range(15, 0, -1):
            d_copy(th, slot).start()

    def finish(th):
        own_d[th].wait()
        for slot in range(1, 16):
            pltpu.make_async_remote_copy(
                src_ref=answer.at[th, 0], dst_ref=back.at[th, t_peer(t_me, slot)],
                send_sem=d_send.at[th, slot], recv_sem=d_recv.at[th, slot],
                device_id={"tm": t_peer(t_me, slot)}, device_id_type=MESH,
            ).wait_recv()
        moved = dot(unperm[...], back[th].reshape(256, WIDTH)).astype(BF16)
        out[:, th * 16:th * 16 + 16, :] = moved.reshape(16, 16, WIDTH)

    pl.semaphore_wait(y_sem, 2)
    pl.semaphore_wait(x_sem, 2)
    for slot in Y_STEPS:
        pl.semaphore_signal(all_sem, inc=1, device_id={"tm": t_peer(t_me, slot)}, device_id_type=MESH)
    for th in range(2):
        space_block(th, 0)
        space_block(th, 1)
    loads[1].wait()
    pl.semaphore_wait(all_sem, 3)
    regroup(0, 0)
    time_project(0, 0)
    regroup(0, 1)
    regroup(1, 0)
    time_project(0, 1)
    regroup(1, 1)
    time_block(0, 0)
    time_block(0, 1)
    send_answer(0)
    time_project(1, 0)
    time_project(1, 1)
    time_block(1, 0)
    time_block(1, 1)
    send_answer(1)
    finish(0)
    finish(1)

    for near in range(8):
        for dest in (core, 1 - core):
            if near != HERE or dest is not core:
                a_copy(near, dest).wait_send()
                b_copy(0, near, dest).wait_send()
                b_copy(1, near, dest).wait_send()
    for slot in range(1, 16):
        for th in range(2):
            for part in range(2):
                c_copy(th, part, slot).wait_send()
            d_copy(th, slot).wait_send()


def on_device(clip, w_spatial, w_temporal):
    dma = pltpu.SemaphoreType.DMA
    vmem = pltpu.VMEM
    return pl.pallas_call(
        kernel,
        out_shape=jax.ShapeDtypeStruct(clip.shape, BF16),
        in_specs=[pl.BlockSpec(memory_space=pltpu.HBM)] * 3,
        out_specs=pl.BlockSpec(memory_space=pltpu.VMEM),
        scratch_shapes=[
            vmem((4, WIDTH, WIDTH), BF16),
            vmem((4, WIDTH, WIDTH), BF16),
            vmem((2, 8, 32, WIDTH), BF16),
            vmem((PAIRS, 2, 512, LANES), BF16),
            vmem((PAIRS, 512, LANES), BF16),
            vmem((PAIRS, 512, 2 * LANES), BF16),
            vmem((128, WIDTH), BF16),
            vmem((2, 2, 8, 16, WIDTH), BF16),
            vmem((2, 2, 8, 16, WIDTH), BF16),
            vmem((128, 128), BF16),
            vmem((256, 256), BF16),
            vmem((256, 128), F32),
            vmem((256, 256), F32),
            vmem((2, 2, 16, 8, WIDTH), BF16),
            vmem((2, 2, 16, 8, WIDTH), BF16),
            vmem((PAIRS, 2, 2, 128, LANES), BF16),
            vmem((PAIRS, 2, 128, LANES), BF16),
            vmem((PAIRS, 2, 128, 2 * LANES), BF16),
            vmem((256, WIDTH), BF16),
            vmem((2, 16, 16, WIDTH), BF16),
            vmem((2, 16, 16, WIDTH), BF16),
            dma((2,)),
            dma((2, 8)), dma((2, 8)),
            dma((2, 2, 8)), dma((2, 2, 8)),
            dma((2, 2, 16)), dma((2, 2, 16)),
            dma((2, 16)), dma((2, 16)),
            dma((9,)),
            pltpu.SemaphoreType.REGULAR,
            pltpu.SemaphoreType.REGULAR,
            pltpu.SemaphoreType.REGULAR,
        ],
        compiler_params=pltpu.CompilerParams(
            collective_id=0, has_side_effects=True, vmem_limit_bytes=40 * 1024 * 1024
        ),
    )(*(pltpu.with_memory_space_constraint(v, pltpu.HBM) for v in (clip, w_spatial, w_temporal)))


def solution(mesh):
    placed = (P("tm", "space", None), P(), P())
    return jax.shard_map(
        on_device, mesh=mesh, in_specs=placed, out_specs=P("tm", "space", None), check_vma=False
    )
```
